256 devices in a mesh: dom: 32 (over y_lo, z, core), repl: 8 (over y_hi, x).
Axes of the slice: x: 4, y: 4 (y_hi: 2, y_lo: 2; y = y_hi * 2 + y_lo), z: 8, core: 2. Of those that a mesh axis runs over, the one named last changes fastest.
Arguments:
- features: float32 [131072, 256], P(('dom', 'repl')), may hold values from -6 to 6
- weight: bfloat16 [256, 256], replicated, may hold values from -0.375 to 0.375
- bias_vector: float32 [256], replicated, may hold values from -0.5 to 0.5
- cotangent: bfloat16 [131072, 256], P(('dom', 'repl')), may hold values from -6 to 6
- near_tiles: bfloat16 [4096, 128, 128], P(('dom', 'repl')), may hold values from -0.1875 to 0.1875
- near_offsets: int32 [256, 33], P(('dom', 'repl')), may hold values from 0 to 16, as said below
- near_cols: int32 [256, 16], P(('dom', 'repl')), may hold values from 0 to 3, as said below
- far_tiles: bfloat16 [256, 32, 1, 128, 128], P(('dom', 'repl')), may hold values from -0.1875 to 0.1875
- far_rows: int32 [256, 32, 1], P(('dom', 'repl')), may hold values from -1 to 31, as said below
- far_cols: int32 [256, 32, 1], P(('dom', 'repl')), may hold values from 0 to 3
Outputs:
- hidden: bfloat16 [131072, 256], P(('dom', 'repl'))
- grad_features: float32 [131072, 256], P(('dom', 'repl'))
- weight_grad: float32 [256, 256], replicated
The draws below stay inside these ranges and needn't reach their ends.
Inputs may be any that keep to these rules, and one draw needn't show every extreme that they name: `near_offsets`: each row is non-decreasing, begins with 0 and ends with 16. `near_cols`: within one tile row of one device the near tiles' columns differ and rise. `far_rows`: -1 marks an empty slot. A device's slots for the groups whose index of dom lies at most 2 steps from its own around the cycle are never empty.
All inputs are finite; a program needn't handle non-finite values.
Results may differ from the reference program's by a relative error of at most 0.0075.
Values may be sent and summed in bfloat16 or wider, within the bound.
No kernel may reach another device: no remote copies, remote signals or barrier semaphores. Data moves between devices by JAX's collectives and lax.ppermute only.
A program may use at most 128 MiB of HBM per device.

```python
import math
import jax
import jax.numpy as jnp
from jax import lax

FEAT = 256
BLOCK = 128
CAP = 1
RB_DEV = 4
RB_DOM = 32
NEAR = 16
SHARDS = 256
NODES = 131072
N_DOM = 32
N_REPL = 8


def near_pattern(key):
    base_key = jax.random.fold_in(key, 7)

    def one_shard(shard_index):
        shard_key = jax.random.fold_in(base_key, shard_index)
        picked = jnp.sort(jax.random.permutation(shard_key, RB_DOM * RB_DEV)[:NEAR].astype(jnp.int32))
        row_ids = picked // RB_DEV
        col_ids = picked % RB_DEV
        row_counts = jnp.sum((row_ids[None, :] == jnp.arange(RB_DOM, dtype=jnp.int32)[:, None]).astype(jnp.int32), axis=1)
        offsets = jnp.concatenate([jnp.zeros((1,), jnp.int32), jnp.cumsum(row_counts).astype(jnp.int32)])
        return (offsets, col_ids)
    return jax.vmap(one_shard)(jnp.arange(SHARDS, dtype=jnp.int32))


def draw_near_offsets(key, part):
    return near_pattern(key)[0]


def draw_near_cols(key, part):
    return near_pattern(key)[1]


def draw_far_rows(key, part):
    base_key = jax.random.fold_in(key, 11)
    keep_key = jax.random.fold_in(base_key, 1)
    row_key = jax.random.fold_in(base_key, 2)
    shard_ids = jnp.arange(SHARDS, dtype=jnp.int32)[:, None, None]
    group_ids = jnp.arange(N_DOM, dtype=jnp.int32)[None, :, None]
    own_group = shard_ids // N_REPL
    apart = jnp.abs(group_ids - own_group)
    cycle_gap = jnp.minimum(apart, N_DOM - apart)
    lucky = jax.random.randint(keep_key, (SHARDS, N_DOM, CAP), 0, 4, dtype=jnp.int32) == 0
    keep = jnp.logical_or(cycle_gap <= N_DOM // 16, lucky)
    rows = jax.random.randint(row_key, (SHARDS, N_DOM, CAP), 0, RB_DOM, dtype=jnp.int32)
    forced = jnp.logical_and(shard_ids == 0, group_ids == 0)
    rows = jnp.where(forced, RB_DOM - 1, rows)
    return jnp.where(keep, rows, -1).astype(jnp.int32)


def place_ends(entries, rng, least, top_value):
    longest = entries.shape.index(max(entries.shape))
    spots = []
    for shift in (0, 1):
        where = [jax.random.randint(jax.random.fold_in(rng, axis), (), 0, length) for axis, length in enumerate(entries.shape)]
        where[longest] = (where[longest] + shift) % entries.shape[longest]
        spots.append(tuple(where))
    return entries.at[spots[0]].set(least).at[spots[1]].set(top_value)


def steps_of(stream_key, dims, cuts, least, high):
    def one(position, shards_of):
        steps = jax.random.uniform(jax.random.fold_in(jax.random.fold_in(stream_key, 6), position), (shards_of,), jnp.float32, least / len(cuts), high / len(cuts))
        return jnp.repeat(jnp.exp(steps), dims[position] // shards_of).reshape((-1,) + (1,) * (len(dims) - position - 1))

    gain = one(*cuts[0])
    for cut in cuts[1:]:
        gain = gain * one(*cut)
    return gain


def centred(rng, shape, spread, limit, pieces=(), kind=jnp.bfloat16):
    array = spread * jax.random.normal(rng, shape, jnp.float32)
    if pieces:
        array = array * steps_of(rng, shape, pieces, -0.22, 0.18)
    return jnp.clip(array, -limit, limit).astype(kind)


def setup_inputs(seed: int = 0) -> dict:
    keys = jax.random.split(jax.random.key(seed), 11)
    return {
        "features": centred(keys[0], (NODES, FEAT), 1.0, 6.0, ((0, 256),), jnp.float32),
        "weight": centred(keys[1], (FEAT, FEAT), FEAT ** -0.5, 0.375),
        "bias_vector": jnp.clip(jax.random.uniform(keys[2], (FEAT,), jnp.float32, -0.5, 0.5), -0.5, 0.5),
        "cotangent": centred(keys[3], (NODES, FEAT), 1.0, 6.0, ((0, 256),)),
        "near_tiles": centred(keys[4], (SHARDS * NEAR, BLOCK, BLOCK), (BLOCK * (NEAR + N_DOM * CAP // 2) // RB_DEV) ** -0.5, 0.1875, ((0, 256),)),
        "near_offsets": draw_near_offsets(jax.random.fold_in(keys[10], 71), 0),
        "near_cols": draw_near_cols(jax.random.fold_in(keys[10], 71), 0),
        "far_tiles": centred(keys[7], (SHARDS, N_DOM, CAP, BLOCK, BLOCK), (BLOCK * (NEAR + N_DOM * CAP // 2) // RB_DEV) ** -0.5, 0.1875, ((0, 256),)),
        "far_rows": draw_far_rows(jax.random.fold_in(keys[10], 71), 0),
        "far_cols": place_ends(jax.random.randint(keys[9], (SHARDS, N_DOM, CAP), 0, RB_DEV), jax.random.fold_in(keys[9], 1), 0, RB_DEV - 1).astype(jnp.int32),
    }


def membership_flags(index, extent):
    return (index[..., None] == jnp.arange(extent, dtype=jnp.int32)).astype(jnp.float32)

def slot_rows(offsets):
    slots = jnp.arange(NEAR, dtype=jnp.int32)
    return lax.optimization_barrier(jnp.sum((offsets[1:, None] <= slots[None, :]).astype(jnp.int32), axis=0))

def matrix_result(form, left, right):
    return jnp.einsum(form, left, right, precision=lax.Precision.HIGHEST)

def activation_grad(pre_values, upstream):
    sigma = jax.nn.sigmoid(pre_values)
    return (upstream.astype(jnp.float32) * sigma * (1.0 + pre_values * (1.0 - sigma))).astype(jnp.bfloat16)

def reference(features, weight, bias_vector, cotangent, near_tiles, near_offsets, near_cols, far_tiles, far_rows, far_cols):
    reduced = features.astype(jnp.bfloat16)
    lanes = reduced.astype(jnp.float32).reshape(N_DOM, N_REPL, RB_DEV, BLOCK, FEAT)
    near_all = near_tiles.reshape(SHARDS, NEAR, BLOCK, BLOCK)

    def shard_parts(shard_index):
        dom_index = shard_index // N_REPL
        lane_index = shard_index % N_REPL
        nearby_square_tile = lax.dynamic_index_in_dim(near_all, shard_index, 0, keepdims=False).astype(jnp.float32)
        offsets = lax.dynamic_index_in_dim(near_offsets, shard_index, 0, keepdims=False)
        near_col = lax.dynamic_index_in_dim(near_cols, shard_index, 0, keepdims=False)
        far_tile = lax.dynamic_index_in_dim(far_tiles, shard_index, 0, keepdims=False).astype(jnp.float32)
        far_row = lax.dynamic_index_in_dim(far_rows, shard_index, 0, keepdims=False)
        far_col = lax.dynamic_index_in_dim(far_cols, shard_index, 0, keepdims=False)
        return (dom_index, lane_index, nearby_square_tile, membership_flags(slot_rows(offsets), RB_DOM), membership_flags(near_col, RB_DEV), far_tile, membership_flags(far_row, RB_DOM), membership_flags(far_col, RB_DEV))

    def forward_step(running, shard_index):
        dom_index, lane_index, nearby_square_tile, nearby_row_onehot, nearby_column_onehot, far_tile, far_row_hot, far_col_hot = shard_parts(shard_index)
        lane_blocks = lax.dynamic_index_in_dim(lanes, lane_index, 1, keepdims=False)
        local_block_list = lax.dynamic_index_in_dim(lane_blocks, dom_index, 0, keepdims=False)
        nearby_input_rows = matrix_result('el,lxh->exh', nearby_column_onehot, local_block_list)
        partial_sum = matrix_result('qr,qaf->raf', nearby_row_onehot, matrix_result('qab,qbf->qaf', nearby_square_tile, nearby_input_rows))
        far_inputs = matrix_result('kqc,kcbf->kqbf', far_col_hot, lane_blocks)
        partial_sum = partial_sum + matrix_result('kqr,kqaf->raf', far_row_hot, matrix_result('kqab,kqbf->kqaf', far_tile, far_inputs))
        current = lax.dynamic_index_in_dim(running, dom_index, 0, keepdims=False)
        running = lax.dynamic_update_index_in_dim(running, current + partial_sum, dom_index, 0)
        return (running, None)
    start_sum = jnp.zeros((N_DOM, RB_DOM, BLOCK, FEAT), jnp.float32)
    totals = lax.scan(forward_step, start_sum, jnp.arange(SHARDS, dtype=jnp.int32))[0]
    summed = totals.reshape(NODES, FEAT).astype(jnp.bfloat16)
    pre_act = jnp.dot(summed, weight, preferred_element_type=jnp.float32) + bias_vector
    hidden = jax.nn.silu(pre_act).astype(jnp.bfloat16)
    grad_pre = activation_grad(pre_act, cotangent)
    weight_grad = jnp.dot(summed.T, grad_pre, preferred_element_type=jnp.float32) * (1.0 / math.sqrt(NODES))
    grad_rows = jnp.dot(grad_pre, weight.T, preferred_element_type=jnp.float32).astype(jnp.bfloat16)
    grad_groups = grad_rows.astype(jnp.float32).reshape(N_DOM, RB_DOM, BLOCK, FEAT)

    def backward_step(running, shard_index):
        dom_index, lane_index, nearby_square_tile, nearby_row_onehot, nearby_column_onehot, far_tile, far_row_hot, far_col_hot = shard_parts(shard_index)
        cluster_block_list = lax.dynamic_index_in_dim(grad_groups, dom_index, 0, keepdims=False)
        nearby_output_rows = matrix_result('ml,mrx->lrx', nearby_column_onehot, matrix_result('ltp,ltk->lpk', nearby_square_tile, matrix_result('om,mgh->ogh', nearby_row_onehot, cluster_block_list)))
        far_out = matrix_result('kqc,kqbf->kcbf', far_col_hot, matrix_result('kqab,kqaf->kqbf', far_tile, matrix_result('kqr,rbf->kqbf', far_row_hot, cluster_block_list)))
        own_slot = lax.dynamic_index_in_dim(far_out, dom_index, 0, keepdims=False) + nearby_output_rows
        far_out = lax.dynamic_update_index_in_dim(far_out, own_slot, dom_index, 0)
        current = lax.dynamic_index_in_dim(running, lane_index, 1, keepdims=False)
        running = lax.dynamic_update_index_in_dim(running, current + far_out, lane_index, 1)
        return (running, None)
    grad_start = jnp.zeros((N_DOM, N_REPL, RB_DEV, BLOCK, FEAT), jnp.float32)
    grad_features = lax.scan(backward_step, grad_start, jnp.arange(SHARDS, dtype=jnp.int32))[0].reshape(NODES, FEAT)
    return (hidden, grad_features, weight_grad)
```

```python
import math

import jax
import jax.numpy as jnp
from jax import lax
from jax.experimental import pallas as pl
from jax.experimental.pallas import tpu as pltpu
from jax.sharding import PartitionSpec as P

BF16 = jnp.bfloat16
F32 = jnp.float32
STEP = 8


def slot_rows(offsets, slot_count):
    slots = jnp.arange(slot_count, dtype=jnp.int32)
    return jnp.sum((offsets[1:, None] <= slots[None, :]).astype(jnp.int32), axis=0)


def smem():
    return pl.BlockSpec(memory_space=pltpu.SMEM)


def whole(shape):
    return pl.BlockSpec(shape, lambda i: (0,) * len(shape))


def stepped(shape):
    return pl.BlockSpec(shape, lambda i: (i,) + (0,) * (len(shape) - 1))


def params(mib=40):
    return pltpu.CompilerParams(
        dimension_semantics=("arbitrary",), vmem_limit_bytes=mib * 1024 * 1024
    )


def transposed_dot(left, right):
    return lax.dot_general(left, right, (((0,), (0,)), ((), ())), preferred_element_type=F32)


def pick_blocks(wanted, features, dom_count, tile):
    rows, width = features.shape

    def kernel(wanted_ref, feat_ref, out_ref, red_ref):
        step = pl.program_id(0)

        @pl.when(step == 0)
        def _():
            red_ref[...] = feat_ref[...].astype(BF16)

        for j in range(STEP):
            at = pl.multiple_of(wanted_ref[step * STEP + j] * tile, tile)
            out_ref[j] = red_ref[pl.ds(at, tile), :]

    return pl.pallas_call(
        kernel,
        grid=(dom_count // STEP,),
        in_specs=[smem(), whole((rows, width))],
        out_specs=[stepped((STEP, tile, width)), whole((rows, width))],
        out_shape=[
            jax.ShapeDtypeStruct((dom_count, tile, width), BF16),
            jax.ShapeDtypeStruct((rows, width), BF16),
        ],
        compiler_params=params(),
        name="pick_blocks",
    )(wanted, features)


def aggregate(far_rows, near_rows, near_cols, arrived, far_tiles, near_tiles, reduced, blocks_dom):
    dom_count, tile, width = arrived.shape
    near_count = near_tiles.shape[0]
    steps = dom_count // STEP

    def kernel(frow_ref, nrow_ref, ncol_ref, in_ref, far_ref, near_ref, red_ref, out_ref, acc_ref):
        step = pl.program_id(0)

        def add(row, value):
            at = pl.ds(pl.multiple_of(row * tile, tile), tile)
            acc_ref[at, :] += value

        @pl.when(step == 0)
        def _():
            acc_ref[...] = jnp.zeros_like(acc_ref)
            for q in range(near_count):
                src = pl.ds(pl.multiple_of(ncol_ref[q] * tile, tile), tile)
                add(
                    nrow_ref[q],
                    jnp.dot(near_ref[q], red_ref[src, :], preferred_element_type=F32),
                )

        for j in range(STEP):
            row = frow_ref[step * STEP + j]
            row = jnp.where(row < 0, blocks_dom, row)
            add(row, jnp.dot(far_ref[j], in_ref[j], preferred_element_type=F32))

        @pl.when(step == steps - 1)
        def _():
            out_ref[...] = acc_ref[: blocks_dom * tile, :].astype(BF16)

    return pl.pallas_call(
        kernel,
        grid=(steps,),
        in_specs=[
            smem(),
            smem(),
            smem(),
            stepped((STEP, tile, width)),
            stepped((STEP, tile, tile)),
            whole((near_count, tile, tile)),
            whole(reduced.shape),
        ],
        out_specs=whole((blocks_dom * tile, width)),
        out_shape=jax.ShapeDtypeStruct((blocks_dom * tile, width), BF16),
        scratch_shapes=[pltpu.VMEM(((blocks_dom + 1) * tile, width), F32)],
        compiler_params=params(),
        name="aggregate",
    )(far_rows, near_rows, near_cols, arrived, far_tiles, near_tiles, reduced)


def dense_stage(parts, weight, bias, cotangent):
    peers, rows, width = parts.shape
    chunk = 256

    def kernel(parts_ref, w_ref, b_ref, ct_ref, hid_ref, grads_ref, wt_ref):
        step = pl.program_id(0)
        total = parts_ref[0].astype(F32)
        for j in range(1, peers):
            total = total + parts_ref[j].astype(F32)
        summed = total.astype(BF16)
        w = w_ref[...]
        pre = jnp.dot(summed, w, preferred_element_type=F32) + b_ref[...]
        sigma = jax.nn.sigmoid(pre)
        hid_ref[...] = (pre * sigma).astype(BF16)
        grad_pre = (ct_ref[...].astype(F32) * sigma * (1.0 + pre * (1.0 - sigma))).astype(BF16)
        grad_rows = lax.dot_general(
            grad_pre, w, (((1,), (1,)), ((), ())), preferred_element_type=F32
        ).astype(BF16)
        for j in range(peers):
            grads_ref[j] = grad_rows
        term = transposed_dot(summed, grad_pre)

        @pl.when(step == 0)
        def _():
            wt_ref[...] = term

        @pl.when(step != 0)
        def _():
            wt_ref[...] += term

    return pl.pallas_call(
        kernel,
        grid=(rows // chunk,),
        in_specs=[
            pl.BlockSpec((peers, chunk, width), lambda i: (0, i, 0)),
            whole(weight.shape),
            whole((1, width)),
            stepped((chunk, width)),
        ],
        out_specs=[
            stepped((chunk, width)),
            pl.BlockSpec((peers, chunk, width), lambda i: (0, i, 0)),
            whole((width, width)),
        ],
        out_shape=[
            jax.ShapeDtypeStruct((rows, width), BF16),
            jax.ShapeDtypeStruct((peers, rows, width), BF16),
            jax.ShapeDtypeStruct((width, width), F32),
        ],
        compiler_params=params(),
        name="dense_stage",
    )(parts, weight, bias, cotangent)


def far_terms(far_rows, group_grad, far_tiles, tile):
    dom_count = far_tiles.shape[0]
    width = group_grad.shape[1]

    def kernel(frow_ref, grad_ref, far_ref, out_ref):
        step = pl.program_id(0)
        for j in range(STEP):
            row = frow_ref[step * STEP + j]
            at = pl.ds(pl.multiple_of(jnp.maximum(row, 0) * tile, tile), tile)
            term = transposed_dot(far_ref[j], grad_ref[at, :])
            out_ref[j] = jnp.where(row >= 0, term, 0.0).astype(BF16)

    return pl.pallas_call(
        kernel,
        grid=(dom_count // STEP,),
        in_specs=[smem(), whole(group_grad.shape), stepped((STEP, tile, tile))],
        out_specs=stepped((STEP, tile, width)),
        out_shape=jax.ShapeDtypeStruct((dom_count, tile, width), BF16),
        compiler_params=params(),
        name="far_terms",
    )(far_rows, group_grad, far_tiles)


def near_terms(near_rows, near_cols, group_grad, near_tiles, rows_dev):
    near_count, tile, _ = near_tiles.shape
    width = group_grad.shape[1]

    def kernel(nrow_ref, ncol_ref, grad_ref, near_ref, out_ref):
        out_ref[...] = jnp.zeros_like(out_ref)
        for q in range(near_count):
            src = pl.ds(pl.multiple_of(nrow_ref[q] * tile, tile), tile)
            dst = pl.ds(pl.multiple_of(ncol_ref[q] * tile, tile), tile)
            out_ref[dst, :] += transposed_dot(near_ref[q], grad_ref[src, :])

    return pl.pallas_call(
        kernel,
        grid=(1,),
        in_specs=[smem(), smem(), whole(group_grad.shape), whole(near_tiles.shape)],
        out_specs=whole((rows_dev, width)),
        out_shape=jax.ShapeDtypeStruct((rows_dev, width), F32),
        compiler_params=params(),
        name="near_terms",
    )(near_rows, near_cols, group_grad, near_tiles)


def place_terms(wanted, arrived, local):
    dom_count, tile, width = arrived.shape

    def kernel(wanted_ref, in_ref, local_ref, out_ref):
        step = pl.program_id(0)

        @pl.when(step == 0)
        def _():
            out_ref[...] = local_ref[...]

        for j in range(STEP):
            at = pl.ds(pl.multiple_of(wanted_ref[step * STEP + j] * tile, tile), tile)
            out_ref[at, :] += in_ref[j].astype(F32)

    return pl.pallas_call(
        kernel,
        grid=(dom_count // STEP,),
        in_specs=[smem(), stepped((STEP, tile, width)), whole(local.shape)],
        out_specs=whole(local.shape),
        out_shape=jax.ShapeDtypeStruct(local.shape, F32),
        compiler_params=params(),
        name="place_terms",
    )(wanted, arrived, local)


def exchange(values, axes):
    return lax.all_to_all(values, axes, 0, 0, tiled=True)


def on_device(
    features,
    weight,
    bias_vector,
    cotangent,
    near_tiles,
    near_offsets,
    near_cols,
    far_tiles,
    far_rows,
    far_cols,
):
    rows_dev, width = features.shape
    tile = near_tiles.shape[1]
    dom_count = lax.axis_size("dom")
    repl_count = lax.axis_size("repl")
    blocks_dom = rows_dev // tile * repl_count
    tiles = far_tiles.reshape(dom_count, tile, tile)
    frow = far_rows.reshape(dom_count)
    fcol = far_cols.reshape(dom_count)
    ncol = near_cols[0]
    nrow = slot_rows(near_offsets[0], near_tiles.shape[0])

    wanted = exchange(jnp.broadcast_to(fcol[:, None], (dom_count, 128)), "dom")[:, 0]
    blocks, reduced = pick_blocks(wanted, features, dom_count, tile)
    arrived = exchange(blocks, "dom")
    partial = aggregate(frow, nrow, ncol, arrived, tiles, near_tiles, reduced, blocks_dom)
    parts = exchange(partial.reshape(repl_count, rows_dev, width), "repl")
    hidden, grads, weight_term = dense_stage(parts, weight, bias_vector.reshape(1, width), cotangent)

    group_grad = exchange(grads, "repl").reshape(blocks_dom * tile, width)
    terms = far_terms(frow, group_grad, tiles, tile)
    far_back = exchange(terms, "dom")

    device_count = dom_count * repl_count
    node_total = rows_dev * device_count
    per_device = width // device_count
    gathered = exchange(weight_term, ("dom", "repl")).reshape(device_count, per_device * width)
    total = jnp.sum(gathered, axis=0, keepdims=True) * (1.0 / math.sqrt(node_total))
    spread = jnp.broadcast_to(total, (device_count, per_device * width))
    weight_grad = exchange(spread, ("dom", "repl")).reshape(width, width)

    local = near_terms(nrow, ncol, group_grad, near_tiles, rows_dev)
    grad_features = place_terms(wanted, far_back, local)
    return (hidden, grad_features, weight_grad)


def solution(mesh):
    placed = (
        P(("dom", "repl"), None),
        P(),
        P(),
        P(("dom", "repl"), None),
        P(("dom", "repl"), None, None),
        P(("dom", "repl"), None),
        P(("dom", "repl"), None),
        P(("dom", "repl"), None, None, None, None),
        P(("dom", "repl"), None, None),
        P(("dom", "repl"), None, None),
    )
    return jax.shard_map(
        on_device,
        mesh=mesh,
        in_specs=placed,
        out_specs=(P(("dom", "repl"), None), P(("dom", "repl"), None), P()),
        check_vma=False,
    )
```

```python
import math

import jax
import jax.numpy as jnp
from jax import lax
from jax.experimental import pallas as pl
from jax.experimental.pallas import tpu as pltpu
from jax.sharding import PartitionSpec as P


BF16 = jnp.bfloat16
F32 = jnp.float32
STEP = 8


def slot_rows(offsets, slot_count):
    slots = jnp.arange(slot_count, dtype=jnp.int32)
    return jnp.sum((offsets[1:, None] <= slots[None, :]).astype(jnp.int32), axis=0)


def smem():
    return pl.BlockSpec(memory_space=pltpu.SMEM)


def whole(shape):
    return pl.BlockSpec(shape, lambda i: (0,) * len(shape))


def stepped(shape):
    return pl.BlockSpec(shape, lambda i: (i,) + (0,) * (len(shape) - 1))


def params(mib=40):
    return pltpu.CompilerParams(
        dimension_semantics=("arbitrary",), vmem_limit_bytes=mib * 1024 * 1024
    )


def transposed_dot(left, right):
    return lax.dot_general(left, right, (((0,), (0,)), ((), ())), preferred_element_type=F32)


def hbm():
    return pl.BlockSpec(memory_space=pltpu.HBM)


def in_hbm(values):
    return pltpu.with_memory_space_constraint(values, pltpu.HBM)


def pick_blocks(wanted, reduced, dom_count, tile):
    width = reduced.shape[1]

    def kernel(wanted_ref, red_ref, out_ref, sem):
        copies = []
        for d in range(dom_count):
            at = pl.multiple_of(wanted_ref[d] * tile, tile)
            copy = pltpu.make_async_copy(red_ref.at[pl.ds(at, tile), :], out_ref.at[d], sem.at[d])
            copy.start()
            copies.append(copy)
        for copy in copies:
            copy.wait()

    return pl.pallas_call(
        kernel,
        grid=(1,),
        in_specs=[smem(), whole(reduced.shape)],
        out_specs=hbm(),
        out_shape=pltpu.HBM((dom_count, tile, width), BF16),
        scratch_shapes=[pltpu.SemaphoreType.DMA((dom_count,))],
        compiler_params=params(),
        name="pick_blocks",
    )(wanted, reduced)


def aggregate(far_rows, near_rows, near_cols, arrived, far_tiles, near_tiles, reduced, blocks_dom):
    dom_count, tile, width = arrived.shape
    near_count = near_tiles.shape[0]
    steps = dom_count // STEP

    def kernel(
        frow_ref, nrow_ref, ncol_ref, in_ref, far_ref, near_hbm, red_ref, out_ref, acc_ref, near_ref, sem
    ):
        step = pl.program_id(0)
        fetch = pltpu.make_async_copy(near_hbm, near_ref, sem)

        def add(row, value):
            at = pl.ds(pl.multiple_of(row * tile, tile), tile)
            acc_ref[at, :] += value

        @pl.when(step == 0)
        def _():
            fetch.start()
            acc_ref[...] = jnp.zeros_like(acc_ref)

        for j in range(STEP):
            row = frow_ref[step * STEP + j]
            row = jnp.where(row < 0, blocks_dom, row)
            add(row, jnp.dot(far_ref[j], in_ref[j], preferred_element_type=F32))

        @pl.when(step == steps - 1)
        def _():
            fetch.wait()
            for q in range(near_count):
                src = pl.ds(pl.multiple_of(ncol_ref[q] * tile, tile), tile)
                add(
                    nrow_ref[q],
                    jnp.dot(near_ref[q], red_ref[src, :], preferred_element_type=F32),
                )
            out_ref[...] = acc_ref[: blocks_dom * tile, :].astype(BF16)

    return pl.pallas_call(
        kernel,
        grid=(steps,),
        in_specs=[
            smem(),
            smem(),
            smem(),
            stepped((STEP, tile, width)),
            stepped((STEP, tile, tile)),
            hbm(),
            whole(reduced.shape),
        ],
        out_specs=whole((blocks_dom * tile, width)),
        out_shape=jax.ShapeDtypeStruct((blocks_dom * tile, width), BF16),
        scratch_shapes=[
            pltpu.VMEM(((blocks_dom + 1) * tile, width), F32),
            pltpu.VMEM(near_tiles.shape, BF16),
            pltpu.SemaphoreType.DMA,
        ],
        compiler_params=params(),
        name="aggregate",
    )(far_rows, near_rows, near_cols, arrived, far_tiles, in_hbm(near_tiles), reduced)


def dense_stage(parts, weight, bias, cotangent):
    peers, rows, width = parts.shape
    chunk = 256

    def kernel(parts_ref, w_ref, b_ref, ct_ref, hid_ref, grads_ref, wt_ref, rows_ref, sem):
        step = pl.program_id(0)
        last = rows // chunk - 1
        total = parts_ref[0].astype(F32)
        for j in range(1, peers):
            total = total + parts_ref[j].astype(F32)
        summed = total.astype(BF16)
        w = w_ref[...]
        pre = jnp.dot(summed, w, preferred_element_type=F32) + b_ref[...]
        sigma = jax.nn.sigmoid(pre)
        hid_ref[...] = (pre * sigma).astype(BF16)
        grad_pre = (ct_ref[...].astype(F32) * sigma * (1.0 + pre * (1.0 - sigma))).astype(BF16)
        grad_rows = lax.dot_general(
            grad_pre, w, (((1,), (1,)), ((), ())), preferred_element_type=F32
        ).astype(BF16)
        at = pl.ds(pl.multiple_of(step * chunk, chunk), chunk)
        rows_ref[at, :] = grad_rows
        copies = [
            pltpu.make_async_copy(rows_ref.at[at, :], grads_ref.at[j, at, :], sem.at[step, j])
            for j in range(peers)
        ]
        for copy in copies:
            copy.start()
        term = transposed_dot(summed, grad_pre)

        @pl.when(step == 0)
        def _():
            wt_ref[...] = term

        @pl.when(step != 0)
        def _():
            wt_ref[...] += term

        @pl.when(step == last)
        def _():
            for i in range(last + 1):
                part = pl.ds(i * chunk, chunk)
                for j in range(peers):
                    pltpu.make_async_copy(
                        rows_ref.at[part, :], grads_ref.at[j, part, :], sem.at[i, j]
                    ).wait()

    return pl.pallas_call(
        kernel,
        grid=(rows // chunk,),
        in_specs=[
            pl.BlockSpec((peers, chunk, width), lambda i: (0, i, 0)),
            whole(weight.shape),
            whole((1, width)),
            stepped((chunk, width)),
        ],
        out_specs=[
            stepped((chunk, width)),
            hbm(),
            whole((width, width)),
        ],
        out_shape=[
            jax.ShapeDtypeStruct((rows, width), BF16),
            pltpu.HBM((peers, rows, width), BF16),
            jax.ShapeDtypeStruct((width, width), F32),
        ],
        scratch_shapes=[
            pltpu.VMEM((rows, width), BF16),
            pltpu.SemaphoreType.DMA((rows // chunk, peers)),
        ],
        compiler_params=params(),
        name="dense_stage",
    )(parts, weight, bias, cotangent)


def far_terms(far_rows, group_grad, far_tiles, tile):
    dom_count = far_tiles.shape[0]
    width = group_grad.shape[1]

    def kernel(frow_ref, grad_ref, far_ref, out_ref, terms_ref, sem):
        copies = []
        for k in range(dom_count):
            row = frow_ref[k]
            at = pl.ds(pl.multiple_of(jnp.maximum(row, 0) * tile, tile), tile)
            term = transposed_dot(far_ref[k], grad_ref[at, :])
            terms_ref[k] = jnp.where(row >= 0, term, 0.0).astype(BF16)
            copy = pltpu.make_async_copy(terms_ref.at[k], out_ref.at[k], sem.at[k])
            copy.start()
            copies.append(copy)
        for copy in copies:
            copy.wait()

    return pl.pallas_call(
        kernel,
        grid=(1,),
        in_specs=[smem(), whole(group_grad.shape), whole(far_tiles.shape)],
        out_specs=hbm(),
        out_shape=pltpu.HBM((dom_count, tile, width), BF16),
        scratch_shapes=[
            pltpu.VMEM((dom_count, tile, width), BF16),
            pltpu.SemaphoreType.DMA((dom_count,)),
        ],
        compiler_params=params(),
        name="far_terms",
    )(far_rows, group_grad, far_tiles)


def near_terms(near_rows, near_cols, group_grad, near_tiles, rows_dev):
    near_count, tile, _ = near_tiles.shape
    width = group_grad.shape[1]

    def kernel(nrow_ref, ncol_ref, grad_ref, near_ref, out_ref):
        out_ref[...] = jnp.zeros_like(out_ref)
        for q in range(near_count):
            src = pl.ds(pl.multiple_of(nrow_ref[q] * tile, tile), tile)
            dst = pl.ds(pl.multiple_of(ncol_ref[q] * tile, tile), tile)
            out_ref[dst, :] += transposed_dot(near_ref[q], grad_ref[src, :])

    return pl.pallas_call(
        kernel,
        grid=(1,),
        in_specs=[smem(), smem(), whole(group_grad.shape), whole(near_tiles.shape)],
        out_specs=whole((rows_dev, width)),
        out_shape=pltpu.HBM((rows_dev, width), F32),
        compiler_params=params(),
        name="near_terms",
    )(near_rows, near_cols, group_grad, near_tiles)


def place_terms(wanted, arrived, local):
    dom_count, tile, width = arrived.shape
    steps = dom_count // STEP

    def kernel(wanted_ref, in_ref, local_hbm, out_ref, local_ref, sem):
        step = pl.program_id(0)
        fetch = pltpu.make_async_copy(local_hbm, local_ref, sem)

        @pl.when(step == 0)
        def _():
            fetch.start()
            out_ref[...] = jnp.zeros_like(out_ref)

        for j in range(STEP):
            at = pl.ds(pl.multiple_of(wanted_ref[step * STEP + j] * tile, tile), tile)
            out_ref[at, :] += in_ref[j].astype(F32)

        @pl.when(step == steps - 1)
        def _():
            fetch.wait()
            out_ref[...] += local_ref[...]

    return pl.pallas_call(
        kernel,
        grid=(steps,),
        in_specs=[smem(), stepped((STEP, tile, width)), hbm()],
        out_specs=whole(local.shape),
        out_shape=jax.ShapeDtypeStruct(local.shape, F32),
        scratch_shapes=[pltpu.VMEM(local.shape, F32), pltpu.SemaphoreType.DMA],
        compiler_params=params(),
        name="place_terms",
    )(wanted, in_hbm(arrived), in_hbm(local))


def swap(values, axis, count, bit):
    return lax.ppermute(values, axis, [(i, i ^ bit) for i in range(count)])


def total_over_all(values, scale, dom_count, repl_count):
    place = lax.axis_index("repl")
    bits = []
    bit = repl_count // 2
    while bit:
        bits.append(bit)
        bit //= 2
    for bit in bits:
        half = values.shape[0] // 2
        mine = (place // bit) % 2
        kept = lax.dynamic_slice_in_dim(values, mine * half, half, 0)
        sent = lax.dynamic_slice_in_dim(values, (1 - mine) * half, half, 0)
        values = kept + swap(sent, "repl", repl_count, bit)
    bit = 1
    while bit < dom_count:
        values = values + swap(values, "dom", dom_count, bit)
        bit *= 2
    values = values * scale
    for bit in reversed(bits):
        other = swap(values, "repl", repl_count, bit)
        mine = (place // bit) % 2
        first = jnp.where(mine == 0, values, other)
        second = jnp.where(mine == 0, other, values)
        values = jnp.concatenate([first, second], axis=0)
    return values


def exchange(values, axes):
    return lax.all_to_all(values, axes, 0, 0, tiled=True)


def on_device(
    features,
    weight,
    bias_vector,
    cotangent,
    near_tiles,
    near_offsets,
    near_cols,
    far_tiles,
    far_rows,
    far_cols,
):
    rows_dev, width = features.shape
    tile = near_tiles.shape[1]
    dom_count = lax.axis_size("dom")
    repl_count = lax.axis_size("repl")
    blocks_dom = rows_dev // tile * repl_count
    tiles = far_tiles.reshape(dom_count, tile, tile)
    frow = far_rows.reshape(dom_count)
    fcol = far_cols.reshape(dom_count)
    ncol = near_cols[0]
    nrow = slot_rows(near_offsets[0], near_tiles.shape[0])

    wanted = exchange(jnp.broadcast_to(fcol[:, None], (dom_count, 128)), "dom")[:, 0]
    reduced = features.astype(BF16)
    blocks = pick_blocks(wanted, reduced, dom_count, tile)
    arrived = exchange(blocks, "dom")
    partial = aggregate(frow, nrow, ncol, arrived, tiles, near_tiles, reduced, blocks_dom)
    parts = exchange(partial.reshape(repl_count, rows_dev, width), "repl")
    hidden, grads, weight_term = dense_stage(parts, weight, bias_vector.reshape(1, width), cotangent)

    group_grad = exchange(grads, "repl").reshape(blocks_dom * tile, width)
    terms = far_terms(frow, group_grad, tiles, tile)
    far_back = exchange(terms, "dom")

    node_total = rows_dev * dom_count * repl_count
    weight_grad = total_over_all(weight_term, 1.0 / math.sqrt(node_total), dom_count, repl_count)

    local = near_terms(nrow, ncol, group_grad, near_tiles, rows_dev)
    grad_features = place_terms(wanted, far_back, local)
    return (hidden, grad_features, weight_grad)


def solution(mesh):
    placed = (
        P(("dom", "repl"), None),
        P(),
        P(),
        P(("dom", "repl"), None),
        P(("dom", "repl"), None, None),
        P(("dom", "repl"), None),
        P(("dom", "repl"), None),
        P(("dom", "repl"), None, None, None, None),
        P(("dom", "repl"), None, None),
        P(("dom", "repl"), None, None),
    )
    return jax.shard_map(
        on_device,
        mesh=mesh,
        in_specs=placed,
        out_specs=(P(("dom", "repl"), None), P(("dom", "repl"), None), P()),
        check_vma=False,
    )
```

```python
import math

import jax
import jax.numpy as jnp
from jax import lax
from jax.experimental import pallas as pl
from jax.experimental.pallas import tpu as pltpu
from jax.sharding import PartitionSpec as P


BF16 = jnp.bfloat16
F32 = jnp.float32


def slot_rows(offsets, slot_count):
    slots = jnp.arange(slot_count, dtype=jnp.int32)
    return jnp.sum((offsets[1:, None] <= slots[None, :]).astype(jnp.int32), axis=0)


def smem():
    return pl.BlockSpec(memory_space=pltpu.SMEM)


def whole(shape):
    return pl.BlockSpec(shape, lambda i: (0,) * len(shape))


def stepped(shape):
    return pl.BlockSpec(shape, lambda i: (i,) + (0,) * (len(shape) - 1))


def params(mib=40):
    return pltpu.CompilerParams(
        dimension_semantics=("arbitrary",), vmem_limit_bytes=mib * 1024 * 1024
    )


def transposed_dot(left, right):
    return lax.dot_general(left, right, (((0,), (0,)), ((), ())), preferred_element_type=F32)


def hbm():
    return pl.BlockSpec(memory_space=pltpu.HBM)


def in_hbm(values):
    return pltpu.with_memory_space_constraint(values, pltpu.HBM)


STAGES = ((0, -1, 1), (-2, 2), (-3, 3), (4,))


def anywhere():
    return pl.BlockSpec(memory_space=pl.ANY)


def pick_blocks(place, peer_cols, sources, offsets, z_count, tile):
    width = sources[0].shape[1]
    count = len(offsets)
    peers = peer_cols.shape[0]

    def kernel(place_ref, cols_ref, *refs):
        src, out, sem = refs[:count], refs[count:-1], refs[-1]
        rest, z, core = place_ref[0], place_ref[1], place_ref[2]
        copies = []
        for q in range(peers):
            for n, offset in enumerate(offsets):
                k = rest + lax.rem(z + offset + z_count, z_count) * 2 + core
                at = pl.multiple_of(cols_ref[q, k] * tile, tile)
                copy = pltpu.make_async_copy(
                    src[n].at[pl.ds(at, tile), :], out[q].at[n], sem.at[q, n]
                )
                copy.start()
                copies.append(copy)
        for copy in copies:
            copy.wait()

    return pl.pallas_call(
        kernel,
        grid=(1,),
        in_specs=[smem(), smem()] + [anywhere()] * count,
        out_specs=[anywhere()] * peers,
        out_shape=[jax.ShapeDtypeStruct((count, tile, width), BF16)] * peers,
        scratch_shapes=[pltpu.SemaphoreType.DMA((peers, count))],
        compiler_params=params(),
        name="pick_blocks",
    )(place, peer_cols, *sources)


def aggregate(
    place, far_rows, far_cols, near_rows, near_cols, lane, handed, far_tiles, near_tiles, blocks_dom
):
    tile = near_tiles.shape[1]
    width = lane[0].shape[1]
    near_count = near_tiles.shape[0]
    slots = [(t, n, offset) for t, stage in enumerate(STAGES) for n, offset in enumerate(stage)]
    z_count = len(slots)
    y_stride = 2 * z_count
    rows_out = blocks_dom * tile
    piece = rows_out // 8

    def kernel(place_ref, frow_ref, fcol_ref, nrow_ref, ncol_ref, *refs):
        lane_refs = refs[:z_count]
        hand_refs = refs[z_count : z_count + 3 * len(STAGES)]
        far_ref, near_hbm, out_ref, acc_ref, near_ref, done_ref, sem, out_sem = refs[
            z_count + 3 * len(STAGES) :
        ]
        fetch = pltpu.make_async_copy(near_hbm, near_ref, sem)
        fetch.start()
        acc_ref[...] = jnp.zeros_like(acc_ref)
        rest, z, core = place_ref[0], place_ref[1], place_ref[2]

        def add(row, value):
            at = pl.ds(pl.multiple_of(row * tile, tile), tile)
            acc_ref[at, :] += value

        for m, (t, n, offset) in enumerate(slots):
            for q in range(4):
                line = y_stride - rest if q >= 2 else rest
                side = 1 - core if q % 2 else core
                k = line + lax.rem(z + offset + z_count, z_count) * 2 + side
                if q == 0:
                    at = pl.ds(pl.multiple_of(fcol_ref[k] * tile, tile), tile)
                    block = lane_refs[m][at, :]
                else:
                    block = hand_refs[3 * t + q - 1][n]
                row = frow_ref[k]
                row = jnp.where(row < 0, blocks_dom, row)
                add(row, jnp.dot(far_ref[k], block, preferred_element_type=F32))
        fetch.wait()
        for q in range(near_count):
            at = pl.ds(pl.multiple_of(ncol_ref[q] * tile, tile), tile)
            add(
                nrow_ref[q],
                jnp.dot(near_ref[q], lane_refs[0][at, :], preferred_element_type=F32),
            )
        copies = []
        for n in range(8):
            at = pl.ds(n * piece, piece)
            done_ref[at, :] = acc_ref[at, :].astype(BF16)
            copy = pltpu.make_async_copy(done_ref.at[at, :], out_ref.at[at, :], out_sem.at[n])
            copy.start()
            copies.append(copy)
        for copy in copies:
            copy.wait()

    arrays = [*lane, *handed, far_tiles]
    return pl.pallas_call(
        kernel,
        grid=(1,),
        in_specs=[smem()] * 5 + [whole(a.shape) for a in arrays] + [hbm()],
        out_specs=hbm(),
        out_shape=pltpu.HBM((rows_out, width), BF16),
        scratch_shapes=[
            pltpu.VMEM(((blocks_dom + 1) * tile, width), F32),
            pltpu.VMEM(near_tiles.shape, BF16),
            pltpu.VMEM((rows_out, width), BF16),
            pltpu.SemaphoreType.DMA,
            pltpu.SemaphoreType.DMA((8,)),
        ],
        compiler_params=params(),
        name="aggregate",
    )(place, far_rows, far_cols, near_rows, near_cols, *arrays, in_hbm(near_tiles))


def dense_stage(parts, weight, bias, cotangent):
    peers, rows, width = parts.shape
    chunk = 256

    def kernel(parts_ref, w_ref, b_ref, ct_ref, hid_ref, grads_ref, wt_ref, rows_ref, sem):
        step = pl.program_id(0)
        last = rows // chunk - 1
        total = parts_ref[0].astype(F32)
        for j in range(1, peers):
            total = total + parts_ref[j].astype(F32)
        summed = total.astype(BF16)
        w = w_ref[...]
        pre = jnp.dot(summed, w, preferred_element_type=F32) + b_ref[...]
        sigma = jax.nn.sigmoid(pre)
        hid_ref[...] = (pre * sigma).astype(BF16)
        grad_pre = (ct_ref[...].astype(F32) * sigma * (1.0 + pre * (1.0 - sigma))).astype(BF16)
        grad_rows = lax.dot_general(
            grad_pre, w, (((1,), (1,)), ((), ())), preferred_element_type=F32
        ).astype(BF16)
        at = pl.ds(pl.multiple_of(step * chunk, chunk), chunk)
        rows_ref[at, :] = grad_rows
        copies = [
            pltpu.make_async_copy(rows_ref.at[at, :], grads_ref.at[j, at, :], sem.at[step, j])
            for j in range(peers)
        ]
        for copy in copies:
            copy.start()
        term = transposed_dot(summed, grad_pre)

        @pl.when(step == 0)
        def _():
            wt_ref[...] = term

        @pl.when(step != 0)
        def _():
            wt_ref[...] += term

        @pl.when(step == last)
        def _():
            for i in range(last + 1):
                part = pl.ds(i * chunk, chunk)
                for j in range(peers):
                    pltpu.make_async_copy(
                        rows_ref.at[part, :], grads_ref.at[j, part, :], sem.at[i, j]
                    ).wait()

    return pl.pallas_call(
        kernel,
        grid=(rows // chunk,),
        in_specs=[
            pl.BlockSpec((peers, chunk, width), lambda i: (0, i, 0)),
            whole(weight.shape),
            whole((1, width)),
            stepped((chunk, width)),
        ],
        out_specs=[
            stepped((chunk, width)),
            hbm(),
            whole((width, width)),
        ],
        out_shape=[
            jax.ShapeDtypeStruct((rows, width), BF16),
            pltpu.HBM((peers, rows, width), BF16),
            jax.ShapeDtypeStruct((width, width), F32),
        ],
        scratch_shapes=[
            pltpu.VMEM((rows, width), BF16),
            pltpu.SemaphoreType.DMA((rows // chunk, peers)),
        ],
        compiler_params=params(),
        name="dense_stage",
    )(parts, weight, bias, cotangent)


def far_terms(far_rows, group_grad, far_tiles, tile):
    dom_count = far_tiles.shape[0]
    width = group_grad.shape[1]

    def kernel(frow_ref, grad_ref, far_ref, out_ref, terms_ref, sem):
        copies = []
        for k in range(dom_count):
            row = frow_ref[k]
            at = pl.ds(pl.multiple_of(jnp.maximum(row, 0) * tile, tile), tile)
            term = transposed_dot(far_ref[k], grad_ref[at, :])
            terms_ref[k] = jnp.where(row >= 0, term, 0.0).astype(BF16)
            copy = pltpu.make_async_copy(terms_ref.at[k], out_ref.at[k], sem.at[k])
            copy.start()
            copies.append(copy)
        for copy in copies:
            copy.wait()

    return pl.pallas_call(
        kernel,
        grid=(1,),
        in_specs=[smem(), whole(group_grad.shape), whole(far_tiles.shape)],
        out_specs=hbm(),
        out_shape=pltpu.HBM((dom_count, tile, width), BF16),
        scratch_shapes=[
            pltpu.VMEM((dom_count, tile, width), BF16),
            pltpu.SemaphoreType.DMA((dom_count,)),
        ],
        compiler_params=params(),
        name="far_terms",
    )(far_rows, group_grad, far_tiles)


def near_terms(near_rows, near_cols, group_grad, near_tiles, rows_dev):
    near_count, tile, _ = near_tiles.shape
    width = group_grad.shape[1]

    def kernel(nrow_ref, ncol_ref, grad_ref, near_ref, out_ref):
        out_ref[...] = jnp.zeros_like(out_ref)
        for q in range(near_count):
            src = pl.ds(pl.multiple_of(nrow_ref[q] * tile, tile), tile)
            dst = pl.ds(pl.multiple_of(ncol_ref[q] * tile, tile), tile)
            out_ref[dst, :] += transposed_dot(near_ref[q], grad_ref[src, :])

    return pl.pallas_call(
        kernel,
        grid=(1,),
        in_specs=[smem(), smem(), whole(group_grad.shape), whole(near_tiles.shape)],
        out_specs=whole((rows_dev, width)),
        out_shape=pltpu.HBM((rows_dev, width), F32),
        compiler_params=params(),
        name="near_terms",
    )(near_rows, near_cols, group_grad, near_tiles)


def place_terms(me, group_cols, masks, arrived, local):
    dom_count, tile, _ = arrived.shape

    def kernel(me_ref, cols_ref, in_hbm_ref, local_hbm, out_ref, in_ref, local_ref, sem, in_sem):
        fetch = pltpu.make_async_copy(local_hbm, local_ref, sem)
        fetch.start()
        here = me_ref[0]
        copies = []
        for n, mask in enumerate(masks):
            d = lax.bitwise_xor(here, mask)
            copy = pltpu.make_async_copy(in_hbm_ref.at[d], in_ref.at[n], in_sem.at[n])
            copy.start()
            copies.append(copy)
        out_ref[...] = jnp.zeros_like(out_ref)
        for n in range(dom_count):
            copies[n].wait()
            at = pl.ds(pl.multiple_of(cols_ref[n, here] * tile, tile), tile)
            out_ref[at, :] += in_ref[n].astype(F32)
        fetch.wait()
        out_ref[...] += local_ref[...]

    return pl.pallas_call(
        kernel,
        grid=(1,),
        in_specs=[smem(), smem(), hbm(), hbm()],
        out_specs=whole(local.shape),
        out_shape=jax.ShapeDtypeStruct(local.shape, F32),
        scratch_shapes=[
            pltpu.VMEM(arrived.shape, BF16),
            pltpu.VMEM(local.shape, F32),
            pltpu.SemaphoreType.DMA,
            pltpu.SemaphoreType.DMA((dom_count,)),
        ],
        compiler_params=params(),
        name="place_terms",
    )(me, group_cols, in_hbm(arrived), in_hbm(local))


def swap(values, axis, count, bit):
    return lax.ppermute(values, axis, [(i, i ^ bit) for i in range(count)])


def meet(values, axis, count, bit):
    rounded = lax.reduce_precision(values, 8, 7)
    return rounded + swap(rounded.astype(BF16), axis, count, bit).astype(F32)


def total_over_all(values, scale, dom_count, repl_count):
    core = lax.axis_index("dom") % 2
    half = values.shape[0] // 2
    kept = lax.dynamic_slice_in_dim(values, core * half, half, 0)
    sent = lax.dynamic_slice_in_dim(values, (1 - core) * half, half, 0)
    values = kept + swap(sent, "dom", dom_count, 1)
    bit = 2
    while bit < dom_count // 2:
        values = meet(values, "dom", dom_count, bit)
        bit *= 2
    bit = 1
    while bit < repl_count // 2:
        values = meet(values, "repl", repl_count, bit)
        bit *= 2
    values = meet(values, "dom", dom_count, dom_count // 2)
    values = meet(values, "repl", repl_count, repl_count // 2) * scale
    other = swap(values, "dom", dom_count, 1)
    first = jnp.where(core == 0, values, other)
    second = jnp.where(core == 0, other, values)
    return jnp.concatenate([first, second], axis=0)


def exchange(values, axes):
    return lax.all_to_all(values, axes, 0, 0, tiled=True)


def on_device(
    features,
    weight,
    bias_vector,
    cotangent,
    near_tiles,
    near_offsets,
    near_cols,
    far_tiles,
    far_rows,
    far_cols,
):
    rows_dev, width = features.shape
    tile = near_tiles.shape[1]
    dom_count = lax.axis_size("dom")
    repl_count = lax.axis_size("repl")
    blocks_dom = rows_dev // tile * repl_count
    tiles = far_tiles.reshape(dom_count, tile, tile)
    frow = far_rows.reshape(dom_count)
    fcol = far_cols.reshape(dom_count)
    ncol = near_cols[0]
    nrow = slot_rows(near_offsets[0], near_tiles.shape[0])

    reduced = features.astype(BF16)
    z_count = dom_count // 4
    here = lax.axis_index("dom")
    place = jnp.stack([here // (2 * z_count) * (2 * z_count), here // 2 % z_count, here % 2])

    def along_z(values, shift):
        pairs = [
            (i, i // (2 * z_count) * (2 * z_count) + (i // 2 + shift) % z_count * 2 + i % 2)
            for i in range(dom_count)
        ]
        return lax.ppermute(values, "dom", pairs)

    up = [along_z(reduced, 1)]
    down = [along_z(reduced, -1)]
    masks = (1, dom_count // 2, dom_count // 2 + 1)
    row = jnp.broadcast_to(fcol[None, :], (8, dom_count))
    rows = [swap(row, "dom", dom_count, m)[0] for m in masks]
    peer_cols = jnp.stack(rows)
    for _ in range(2):
        up.append(along_z(up[-1], 1))
        down.append(along_z(down[-1], -1))
    half = rows_dev // 2
    across = [along_z(up[-1][:half], 1), along_z(down[-1][half:], -1)]
    across = jnp.concatenate(across, axis=0)
    lane = (reduced, up[0], down[0], up[1], down[1], up[2], down[2], across)

    def hand_out(first, offsets):
        picked = pick_blocks(
            place, peer_cols, lane[first : first + len(offsets)], offsets, z_count, tile
        )
        return [swap(blocks, "dom", dom_count, m) for blocks, m in zip(picked, masks)]

    handed = []
    first = 0
    for stage in STAGES:
        handed += hand_out(first, stage)
        first += len(stage)
    partial = aggregate(
        place, frow, fcol, nrow, ncol, lane, handed, tiles, near_tiles, blocks_dom
    )
    known = [0, *masks]
    group_cols = jnp.concatenate([fcol[None, :], peer_cols], axis=0)
    bit = 2
    while bit < dom_count // 2:
        other = swap(group_cols, "dom", dom_count, bit)
        group_cols = jnp.concatenate([group_cols, other], axis=0)
        known += [m + bit for m in known]
        bit *= 2
    parts = exchange(partial.reshape(repl_count, rows_dev, width), "repl")
    hidden, grads, weight_term = dense_stage(parts, weight, bias_vector.reshape(1, width), cotangent)

    group_grad = exchange(grads, "repl").reshape(blocks_dom * tile, width)
    terms = far_terms(frow, group_grad, tiles, tile)
    far_back = exchange(terms, "dom")

    node_total = rows_dev * dom_count * repl_count
    weight_grad = total_over_all(weight_term, 1.0 / math.sqrt(node_total), dom_count, repl_count)

    local = near_terms(nrow, ncol, group_grad, near_tiles, rows_dev)
    grad_features = place_terms(here.reshape(1), group_cols, known, far_back, local)
    return (hidden, grad_features, weight_grad)


def solution(mesh):
    placed = (
        P(("dom", "repl"), None),
        P(),
        P(),
        P(("dom", "repl"), None),
        P(("dom", "repl"), None, None),
        P(("dom", "repl"), None),
        P(("dom", "repl"), None),
        P(("dom", "repl"), None, None, None, None),
        P(("dom", "repl"), None, None),
        P(("dom", "repl"), None, None),
    )
    return jax.shard_map(
        on_device,
        mesh=mesh,
        in_specs=placed,
        out_specs=(P(("dom", "repl"), None), P(("dom", "repl"), None), P()),
        check_vma=False,
    )
```

```python
import math

import jax
import jax.numpy as jnp
from jax import lax
from jax.experimental import pallas as pl
from jax.experimental.pallas import tpu as pltpu
from jax.sharding import PartitionSpec as P


BF16 = jnp.bfloat16
F32 = jnp.float32


def slot_rows(offsets, slot_count):
    slots = jnp.arange(slot_count, dtype=jnp.int32)
    return jnp.sum((offsets[1:, None] <= slots[None, :]).astype(jnp.int32), axis=0)


def smem():
    return pl.BlockSpec(memory_space=pltpu.SMEM)


def whole(shape):
    return pl.BlockSpec(shape, lambda i: (0,) * len(shape))


def stepped(shape):
    return pl.BlockSpec(shape, lambda i: (i,) + (0,) * (len(shape) - 1))


def params(mib=40):
    return pltpu.CompilerParams(
        dimension_semantics=("arbitrary",), vmem_limit_bytes=mib * 1024 * 1024
    )


def transposed_dot(left, right):
    return lax.dot_general(left, right, (((0,), (0,)), ((), ())), preferred_element_type=F32)


def hbm():
    return pl.BlockSpec(memory_space=pltpu.HBM)


def in_hbm(values):
    return pltpu.with_memory_space_constraint(values, pltpu.HBM)


STAGES = ((0, -1, 1), (-2, 2), (-3, 3), (4,))


def pick_blocks(place, peer_cols, sources, offsets, z_count, tile):
    width = sources[0].shape[1]
    count = len(offsets)
    peers = peer_cols.shape[0]

    def kernel(place_ref, cols_ref, *refs):
        src, out = refs[:count], refs[count:]
        rest, z, core = place_ref[0], place_ref[1], place_ref[2]
        for q in range(peers):
            for n, offset in enumerate(offsets):
                k = rest + lax.rem(z + offset + z_count, z_count) * 2 + core
                at = pl.multiple_of(cols_ref[q, k] * tile, tile)
                out[q][n] = src[n][pl.ds(at, tile), :]

    return pl.pallas_call(
        kernel,
        grid=(1,),
        in_specs=[smem(), smem()] + [whole(a.shape) for a in sources],
        out_specs=[whole((count, tile, width))] * peers,
        out_shape=[jax.ShapeDtypeStruct((count, tile, width), BF16)] * peers,
        compiler_params=params(),
        name="pick_blocks",
    )(place, peer_cols, *sources)


def aggregate(
    place, far_rows, far_cols, near_rows, near_cols, lane, handed, far_tiles, near_tiles, blocks_dom
):
    tile = near_tiles.shape[1]
    width = lane[0].shape[1]
    near_count = near_tiles.shape[0]
    slots = [(t, n, offset) for t, stage in enumerate(STAGES) for n, offset in enumerate(stage)]
    z_count = len(slots)
    y_stride = 2 * z_count
    rows_out = blocks_dom * tile
    piece = rows_out // 8

    def kernel(place_ref, frow_ref, fcol_ref, nrow_ref, ncol_ref, *refs):
        lane_refs = refs[:z_count]
        hand_refs = refs[z_count : z_count + 3 * len(STAGES)]
        far_ref, near_hbm, out_ref, acc_ref, near_ref, done_ref, sem, out_sem = refs[
            z_count + 3 * len(STAGES) :
        ]
        fetch = pltpu.make_async_copy(near_hbm, near_ref, sem)
        fetch.start()
        acc_ref[...] = jnp.zeros_like(acc_ref)
        rest, z, core = place_ref[0], place_ref[1], place_ref[2]

        def add(row, value):
            at = pl.ds(pl.multiple_of(row * tile, tile), tile)
            acc_ref[at, :] += value

        for m, (t, n, offset) in enumerate(slots):
            for q in range(4):
                line = y_stride - rest if q >= 2 else rest
                side = 1 - core if q % 2 else core
                k = line + lax.rem(z + offset + z_count, z_count) * 2 + side
                if q == 0:
                    at = pl.ds(pl.multiple_of(fcol_ref[k] * tile, tile), tile)
                    block = lane_refs[m][at, :]
                else:
                    block = hand_refs[3 * t + q - 1][n]
                row = frow_ref[k]
                row = jnp.where(row < 0, blocks_dom, row)
                add(row, jnp.dot(far_ref[k], block, preferred_element_type=F32))
        fetch.wait()
        for q in range(near_count):
            at = pl.ds(pl.multiple_of(ncol_ref[q] * tile, tile), tile)
            add(
                nrow_ref[q],
                jnp.dot(near_ref[q], lane_refs[0][at, :], preferred_element_type=F32),
            )
        copies = []
        for n in range(8):
            at = pl.ds(n * piece, piece)
            done_ref[at, :] = acc_ref[at, :].astype(BF16)
            copy = pltpu.make_async_copy(done_ref.at[at, :], out_ref.at[at, :], out_sem.at[n])
            copy.start()
            copies.append(copy)
        for copy in copies:
            copy.wait()

    arrays = [*lane, *handed, far_tiles]
    return pl.pallas_call(
        kernel,
        grid=(1,),
        in_specs=[smem()] * 5 + [whole(a.shape) for a in arrays] + [hbm()],
        out_specs=hbm(),
        out_shape=pltpu.HBM((rows_out, width), BF16),
        scratch_shapes=[
            pltpu.VMEM(((blocks_dom + 1) * tile, width), F32),
            pltpu.VMEM(near_tiles.shape, BF16),
            pltpu.VMEM((rows_out, width), BF16),
            pltpu.SemaphoreType.DMA,
            pltpu.SemaphoreType.DMA((8,)),
        ],
        compiler_params=params(),
        name="aggregate",
    )(place, far_rows, far_cols, near_rows, near_cols, *arrays, in_hbm(near_tiles))


def dense_stage(parts, weight, bias, cotangent):
    peers, rows, width = parts.shape
    chunk = 256

    def kernel(parts_ref, w_ref, b_ref, ct_ref, hid_ref, grads_ref, wt_ref):
        step = pl.program_id(0)
        total = parts_ref[0].astype(F32)
        for j in range(1, peers):
            total = total + parts_ref[j].astype(F32)
        summed = total.astype(BF16)
        w = w_ref[...]
        pre = jnp.dot(summed, w, preferred_element_type=F32) + b_ref[...]
        sigma = jax.nn.sigmoid(pre)
        hid_ref[...] = (pre * sigma).astype(BF16)
        grad_pre = (ct_ref[...].astype(F32) * sigma * (1.0 + pre * (1.0 - sigma))).astype(BF16)
        grad_rows = lax.dot_general(
            grad_pre, w, (((1,), (1,)), ((), ())), preferred_element_type=F32
        ).astype(BF16)
        grads_ref[...] = grad_rows
        term = transposed_dot(summed, grad_pre)

        @pl.when(step == 0)
        def _():
            wt_ref[...] = term

        @pl.when(step != 0)
        def _():
            wt_ref[...] += term

    return pl.pallas_call(
        kernel,
        grid=(rows // chunk,),
        in_specs=[
            pl.BlockSpec((peers, chunk, width), lambda i: (0, i, 0)),
            whole(weight.shape),
            whole((1, width)),
            stepped((chunk, width)),
        ],
        out_specs=[
            stepped((chunk, width)),
            stepped((chunk, width)),
            whole((width, width)),
        ],
        out_shape=[
            jax.ShapeDtypeStruct((rows, width), BF16),
            jax.ShapeDtypeStruct((rows, width), BF16),
            jax.ShapeDtypeStruct((width, width), F32),
        ],
        compiler_params=params(),
        name="dense_stage",
    )(parts, weight, bias, cotangent)


def lay_out(owner_ref, shards, group_ref):
    size = sum(ref.shape[0] for ref in shards[0])
    for n, refs in enumerate(shards):
        start = owner_ref[n] * size
        for ref in refs:
            rows = ref.shape[0]
            group_ref[pl.ds(pl.multiple_of(start, rows), rows), :] = ref[...]
            start = start + rows


def in_pairs(refs, layout):
    taken, out = 0, []
    for count in layout:
        out.append(refs[taken : taken + count])
        taken += count
    return out


def far_terms(far_rows, owners, shards, far_tiles, tile):
    dom_count = far_tiles.shape[0]
    flat = [a for shard in shards for a in shard]
    layout = [len(shard) for shard in shards]
    width = flat[0].shape[1]
    group_rows = sum(a.shape[0] for a in flat)

    def kernel(frow_ref, owner_ref, *refs):
        far_ref, out_ref, terms_ref, grad_ref, sem = refs[len(flat) :]
        lay_out(owner_ref, in_pairs(refs, layout), grad_ref)
        copies = []
        for k in range(dom_count):
            row = frow_ref[k]
            at = pl.ds(pl.multiple_of(jnp.maximum(row, 0) * tile, tile), tile)
            term = transposed_dot(far_ref[k], grad_ref[at, :])
            terms_ref[k] = jnp.where(row >= 0, term, 0.0).astype(BF16)
            copy = pltpu.make_async_copy(terms_ref.at[k], out_ref.at[k], sem.at[k])
            copy.start()
            copies.append(copy)
        for copy in copies:
            copy.wait()

    return pl.pallas_call(
        kernel,
        grid=(1,),
        in_specs=[smem(), smem()] + [whole(a.shape) for a in flat] + [whole(far_tiles.shape)],
        out_specs=hbm(),
        out_shape=pltpu.HBM((dom_count, tile, width), BF16),
        scratch_shapes=[
            pltpu.VMEM((dom_count, tile, width), BF16),
            pltpu.VMEM((group_rows, width), BF16),
            pltpu.SemaphoreType.DMA((dom_count,)),
        ],
        compiler_params=params(),
        name="far_terms",
    )(far_rows, owners, *flat, far_tiles)


def near_terms(near_rows, near_cols, owners, shards, near_tiles, rows_dev):
    near_count, tile, _ = near_tiles.shape
    flat = [a for shard in shards for a in shard]
    layout = [len(shard) for shard in shards]
    width = flat[0].shape[1]
    group_rows = sum(a.shape[0] for a in flat)

    def kernel(nrow_ref, ncol_ref, owner_ref, *refs):
        near_ref, out_ref, grad_ref = refs[len(flat) :]
        lay_out(owner_ref, in_pairs(refs, layout), grad_ref)
        out_ref[...] = jnp.zeros_like(out_ref)
        for q in range(near_count):
            src = pl.ds(pl.multiple_of(nrow_ref[q] * tile, tile), tile)
            dst = pl.ds(pl.multiple_of(ncol_ref[q] * tile, tile), tile)
            out_ref[dst, :] += transposed_dot(near_ref[q], grad_ref[src, :])

    return pl.pallas_call(
        kernel,
        grid=(1,),
        in_specs=[smem()] * 3 + [whole(a.shape) for a in flat] + [whole(near_tiles.shape)],
        out_specs=whole((rows_dev, width)),
        out_shape=pltpu.HBM((rows_dev, width), F32),
        scratch_shapes=[pltpu.VMEM((group_rows, width), BF16)],
        compiler_params=params(),
        name="near_terms",
    )(near_rows, near_cols, owners, *flat, near_tiles)


def place_terms(me, group_cols, masks, arrived, local):
    _, tile, _ = arrived.shape

    def kernel(me_ref, cols_ref, in_ref, local_hbm, out_ref, local_ref, sem):
        fetch = pltpu.make_async_copy(local_hbm, local_ref, sem)
        fetch.start()
        here = me_ref[0]
        out_ref[...] = jnp.zeros_like(out_ref)
        for n, mask in enumerate(masks):
            at = pl.ds(pl.multiple_of(cols_ref[n, here] * tile, tile), tile)
            out_ref[at, :] += in_ref[lax.bitwise_xor(here, mask)].astype(F32)
        fetch.wait()
        out_ref[...] += local_ref[...]

    return pl.pallas_call(
        kernel,
        grid=(1,),
        in_specs=[smem(), smem(), whole(arrived.shape), hbm()],
        out_specs=whole(local.shape),
        out_shape=jax.ShapeDtypeStruct(local.shape, F32),
        scratch_shapes=[pltpu.VMEM(local.shape, F32), pltpu.SemaphoreType.DMA],
        compiler_params=params(),
        name="place_terms",
    )(me, group_cols, pltpu.with_memory_space_constraint(arrived, pltpu.VMEM), in_hbm(local))


def swap(values, axis, count, bit):
    return lax.ppermute(values, axis, [(i, i ^ bit) for i in range(count)])


def gather_group(own, repl_count):
    x_count = repl_count // 2
    half = own.shape[0] // 2

    def along_x(values, shift):
        pairs = [
            (i, i // x_count * x_count + (i + shift) % x_count) for i in range(repl_count)
        ]
        return lax.ppermute(values, "repl", pairs)

    low, high = along_x(own, 1), along_x(own, -1)
    mate = swap(own, "repl", repl_count, x_count)
    far = (along_x(low[:half], 1), along_x(high[half:], -1))
    mate_low, mate_high = along_x(mate, 1), along_x(mate, -1)
    mate_far = (along_x(mate_low[:half], 1), along_x(mate_high[half:], -1))
    shards = ((own,), (low,), (high,), far, (mate,), (mate_low,), (mate_high,), mate_far)
    here = lax.axis_index("repl")
    x, line = here % x_count, here // x_count * x_count
    owners = [start + (x + d) % x_count for start in (line, x_count - line) for d in (0, -1, 1, 2)]
    return shards, jnp.stack(owners)


def meet(values, axis, count, bit):
    rounded = lax.reduce_precision(values, 8, 7)
    return rounded + swap(rounded.astype(BF16), axis, count, bit).astype(F32)


def total_over_all(values, scale, dom_count, repl_count):
    core = lax.axis_index("dom") % 2
    half = values.shape[0] // 2
    kept = lax.dynamic_slice_in_dim(values, core * half, half, 0)
    sent = lax.dynamic_slice_in_dim(values, (1 - core) * half, half, 0)
    values = kept + swap(sent, "dom", dom_count, 1)
    bit = dom_count // 4
    while bit > 1:
        values = meet(values, "dom", dom_count, bit)
        bit //= 2
    bit = 1
    while bit < repl_count // 2:
        values = values + swap(values, "repl", repl_count, bit)
        bit *= 2
    values = values + swap(values, "dom", dom_count, dom_count // 2)
    values = (values + swap(values, "repl", repl_count, repl_count // 2)) * scale
    other = swap(values, "dom", dom_count, 1)
    first = jnp.where(core == 0, values, other)
    second = jnp.where(core == 0, other, values)
    return jnp.concatenate([first, second], axis=0)


def exchange(values, axes):
    return lax.all_to_all(values, axes, 0, 0, tiled=True)


def on_device(
    features,
    weight,
    bias_vector,
    cotangent,
    near_tiles,
    near_offsets,
    near_cols,
    far_tiles,
    far_rows,
    far_cols,
):
    rows_dev, width = features.shape
    tile = near_tiles.shape[1]
    dom_count = lax.axis_size("dom")
    repl_count = lax.axis_size("repl")
    blocks_dom = rows_dev // tile * repl_count
    tiles = far_tiles.reshape(dom_count, tile, tile)
    frow = far_rows.reshape(dom_count)
    fcol = far_cols.reshape(dom_count)
    ncol = near_cols[0]
    nrow = slot_rows(near_offsets[0], near_tiles.shape[0])

    reduced = features.astype(BF16)
    z_count = dom_count // 4
    here = lax.axis_index("dom")
    place = jnp.stack([here // (2 * z_count) * (2 * z_count), here // 2 % z_count, here % 2])

    def along_z(values, shift):
        pairs = [
            (i, i // (2 * z_count) * (2 * z_count) + (i // 2 + shift) % z_count * 2 + i % 2)
            for i in range(dom_count)
        ]
        return lax.ppermute(values, "dom", pairs)

    up = [along_z(reduced, 1)]
    down = [along_z(reduced, -1)]
    masks = (1, dom_count // 2, dom_count // 2 + 1)
    row = jnp.broadcast_to(fcol[None, :], (8, dom_count))
    rows = [swap(row, "dom", dom_count, m)[0] for m in masks]
    peer_cols = jnp.stack(rows)
    for _ in range(2):
        up.append(along_z(up[-1], 1))
        down.append(along_z(down[-1], -1))
    half = rows_dev // 2
    across = [along_z(up[-1][:half], 1), along_z(down[-1][half:], -1)]
    across = jnp.concatenate(across, axis=0)
    lane = (reduced, up[0], down[0], up[1], down[1], up[2], down[2], across)

    def hand_out(first, offsets):
        picked = pick_blocks(
            place, peer_cols, lane[first : first + len(offsets)], offsets, z_count, tile
        )
        return [swap(blocks, "dom", dom_count, m) for blocks, m in zip(picked, masks)]

    handed = []
    first = 0
    for stage in STAGES:
        handed += hand_out(first, stage)
        first += len(stage)
    partial = aggregate(
        place, frow, fcol, nrow, ncol, lane, handed, tiles, near_tiles, blocks_dom
    )
    known = [0, *masks]
    group_cols = jnp.concatenate([fcol[None, :], peer_cols], axis=0)
    bit = 2
    while bit < dom_count // 2:
        other = swap(group_cols, "dom", dom_count, bit)
        group_cols = jnp.concatenate([group_cols, other], axis=0)
        known += [m + bit for m in known]
        bit *= 2
    parts = exchange(partial.reshape(repl_count, rows_dev, width), "repl")
    hidden, grads, weight_term = dense_stage(parts, weight, bias_vector.reshape(1, width), cotangent)

    shards, owners = gather_group(grads, repl_count)
    terms = far_terms(frow, owners, shards, tiles, tile)
    far_back = exchange(terms, "dom")

    node_total = rows_dev * dom_count * repl_count
    weight_grad = total_over_all(weight_term, 1.0 / math.sqrt(node_total), dom_count, repl_count)

    local = near_terms(nrow, ncol, owners, shards, near_tiles, rows_dev)
    grad_features = place_terms(here.reshape(1), group_cols, known, far_back, local)
    return (hidden, grad_features, weight_grad)


def solution(mesh):
    placed = (
        P(("dom", "repl"), None),
        P(),
        P(),
        P(("dom", "repl"), None),
        P(("dom", "repl"), None, None),
        P(("dom", "repl"), None),
        P(("dom", "repl"), None),
        P(("dom", "repl"), None, None, None, None),
        P(("dom", "repl"), None, None),
        P(("dom", "repl"), None, None),
    )
    return jax.shard_map(
        on_device,
        mesh=mesh,
        in_specs=placed,
        out_specs=(P(("dom", "repl"), None), P(("dom", "repl"), None), P()),
        check_vma=False,
    )
```
